128 devices in a mesh: segment: 2 (over z_hi), win: 16 (over y, z_lo, core), head: 4 (over x).
Axes of the slice: x: 4, y: 4, z: 4 (z_hi: 2, z_lo: 2; z = z_hi * 2 + z_lo), core: 2. Of those that a mesh axis runs over, the one named last changes fastest.
Arguments:
- inputs: bfloat16 [2, 30, 480, 1536], P(None, None, 'win', 'head'), may hold values from -16 to 16
- gains: float32 [2, 1536], P('segment'), may hold values from 0.1 to 1.9
- qkv_weight: bfloat16 [2, 1536, 3, 1536], P('segment', None, None, 'head'), may hold values from -3.5 to 3.5
- out_weight: bfloat16 [2, 1536, 1536], P('segment', 'head'), may hold values from -0.15625 to 0.15625
- labels: int32 [30, 480], P(None, 'win'), may hold values from 0 to 3, as said below
Outputs:
- sections: bfloat16 [2, 2, 30, 480, 1536], P('segment', None, None, 'win', 'head')
The draws below stay inside these ranges and needn't reach their ends.
Inputs may be any that keep to these rules, and one draw needn't show every extreme that they name: In each window of 30 by 30 cells the label is 2 on the rows from a drawn row cut on plus 1 on the columns from a drawn column cut on; both cuts lie in 1 to 29, so every window holds all four labels.
All inputs are finite; a program needn't handle non-finite values.
Results may differ from the reference program's by a relative error of at most 0.013.
Values may be sent and summed in bfloat16 or wider, within the bound.
No kernel may reach another device: no remote copies, remote signals or barrier semaphores. Data moves between devices by JAX's collectives and lax.ppermute only.
A program may use at most 128 MiB of HBM per device.

```python
import math
import jax
import jax.numpy as jnp
from jax import lax

D = 1536
HEADS = 12
HEAD_DIM = 128
WIN_SIDE = 30
MB = 2
COLS = 480
N_SEGMENT = 2


def draw_inputs(key, part):
    subkeys = jax.random.split(key, 3)
    full_shape = (MB, WIN_SIDE, COLS, D)
    draws_base = jax.random.normal(subkeys[0], full_shape, jnp.float32)
    row_scale = jnp.exp(jax.random.uniform(subkeys[1], (MB, WIN_SIDE, COLS, 1), jnp.float32, -1.15, 1.15))
    col_scale = jnp.exp(jax.random.uniform(subkeys[2], (D,), jnp.float32, -1.15, 1.15))
    values = draws_base * row_scale * col_scale
    return jnp.clip(values, -16.0, 16.0).astype(jnp.bfloat16)


def draw_qkv_weight(key, part):
    subkeys = jax.random.split(key, 1)
    full_shape = (2, D, 3, D)
    raw_draw = jnp.clip(jax.random.normal(subkeys[0], full_shape, jnp.float32), -6.0, 6.0) / math.sqrt(D)
    slot_gain = jnp.array([1.6, 1.6, 2.0], jnp.float32)[None, None, :, None]
    weights_drawn = raw_draw * slot_gain
    return jnp.clip(weights_drawn, -3.5, 3.5).astype(jnp.bfloat16)


def draw_labels(key, part):
    subkeys = jax.random.split(key, 2)
    win_count = COLS // WIN_SIDE
    row_cut = jax.random.randint(subkeys[0], (win_count,), 1, WIN_SIDE)
    col_cut = jax.random.randint(subkeys[1], (win_count,), 1, WIN_SIDE)
    row_pos = jnp.arange(WIN_SIDE)[:, None]
    col_pos = jnp.arange(COLS)[None, :]
    owner = col_pos // WIN_SIDE
    inner = col_pos % WIN_SIDE
    lower = (row_pos >= row_cut[owner]).astype(jnp.int32)
    right = (inner >= col_cut[owner]).astype(jnp.int32)
    return (2 * lower + right).astype(jnp.int32)


def level_of(rng, shape, cuts, smallest, high):
    loudness = 1.0
    for axis_at, shards_of in cuts:
        draws = jax.random.uniform(jax.random.fold_in(jax.random.fold_in(rng, 6), axis_at), (shards_of,), jnp.float32, smallest / len(cuts), high / len(cuts))
        loudness = loudness * jnp.repeat(jnp.exp(draws), shape[axis_at] // shards_of).reshape((-1,) + (1,) * (len(shape) - 1 - axis_at))
    return loudness


def normal_values(own_key, extent, deviation, most, pieces=(), held_as=jnp.bfloat16):
    factor_of = level_of(own_key, extent, pieces, -0.22, 0.18) if pieces else 1.0
    values = jax.random.normal(own_key, extent, jnp.float32) * deviation * factor_of
    return jnp.minimum(jnp.maximum(values, -most), most).astype(held_as)


def setup_inputs(seed: int = 0) -> dict:
    splits = jax.random.split(jax.random.key(seed), 6)
    return {
        "inputs": draw_inputs(jax.random.fold_in(splits[5], 71), 0),
        "gains": jnp.clip(1.0 + 0.18 * jax.random.normal(splits[1], (N_SEGMENT, D), jnp.float32), 0.1, 1.9),
        "qkv_weight": draw_qkv_weight(jax.random.fold_in(splits[5], 71), 0),
        "out_weight": normal_values(splits[3], (N_SEGMENT, D, D), D ** -0.5, 0.15625, ((0, 2), (1, 4))),
        "labels": draw_labels(jax.random.fold_in(splits[5], 71), 0),
    }


def rms_normed(slab, gain_row):
    values_f = slab.astype(jnp.float32)
    mean_square = lax.optimization_barrier(jnp.mean(values_f * values_f, axis=-1, keepdims=True))
    return (values_f * lax.rsqrt(mean_square + 1e-05) * gain_row).astype(jnp.bfloat16)

def to_windows(grid):
    win_rows = grid.shape[0]
    win_count = grid.shape[1] // win_rows
    features = grid.shape[2]
    return grid.reshape(win_rows, win_count, win_rows, features).transpose(1, 0, 2, 3).reshape(win_count, win_rows * win_rows, features)

def from_windows(blocks, win_rows):
    win_count = blocks.shape[0]
    features = blocks.shape[2]
    return blocks.reshape(win_count, win_rows, win_rows, features).transpose(1, 0, 2, 3).reshape(win_rows, win_count * win_rows, features)

def section_layer(slab, gain_row, wqkv, wout, labels, use_labels):
    normed = rms_normed(slab, gain_row)
    win_normed = to_windows(normed)
    win_labels = to_windows(labels[:, :, None])[:, :, 0]
    flat_qkv = wqkv.reshape(D, 3 * D)

    def one_window(pair):
        normed_win, labels_win = pair
        qkv_all = jnp.dot(normed_win, flat_qkv, preferred_element_type=jnp.float32).astype(jnp.bfloat16)
        qkv_all = qkv_all.reshape(-1, 3, HEADS, HEAD_DIM).astype(jnp.float32)
        queries = qkv_all[:, 0]
        keys_all = qkv_all[:, 1]
        values_all = qkv_all[:, 2]
        scores = jnp.einsum('qhe,khe->hqk', queries, keys_all) * HEAD_DIM ** (-0.5)
        if use_labels:
            allowed = labels_win[:, None] == labels_win[None, :]
            scores = jnp.where(allowed[None], scores, -1e+30)
        top_score = lax.optimization_barrier(jnp.max(scores, axis=-1, keepdims=True))
        expo = jnp.exp(scores - top_score)
        attn_prob = (expo / lax.optimization_barrier(jnp.sum(expo, axis=-1, keepdims=True))).astype(jnp.bfloat16)
        attended = jnp.einsum('hqk,khe->qhe', attn_prob.astype(jnp.float32), values_all).astype(jnp.bfloat16)
        attended = attended.reshape(-1, D)
        return jnp.dot(attended, wout, preferred_element_type=jnp.float32)
    projected = lax.map(one_window, (win_normed, win_labels))
    projected = from_windows(projected, WIN_SIDE)
    return (slab.astype(jnp.float32) + projected).astype(jnp.bfloat16)

def reference(inputs, gains, qkv_weight, out_weight, labels):
    half_cols = WIN_SIDE // 2
    firsts = []
    seconds = []
    for micro in range(MB):
        first = section_layer(inputs[micro], gains[0], qkv_weight[0], out_weight[0], labels, False)
        shifted = jnp.roll(first, -half_cols, axis=1)
        second = section_layer(shifted, gains[1], qkv_weight[1], out_weight[1], labels, True)
        firsts.append(first)
        seconds.append(second)
    return jnp.stack([jnp.stack(firsts), jnp.stack(seconds)])
```

```python
import functools
import math

import jax
import jax.numpy as jnp
from jax import lax
from jax.experimental import pallas as pl
from jax.experimental.pallas import tpu as pltpu
from jax.sharding import PartitionSpec as P


D = 1536
HD = 128
HL = 3
FQ = 384
TS = 240
NT = 4 * TS
HALF = TS // 2
QROWS = 480
AROWS = 480
NEG = -1e30
QSCALE = HD**-0.5 * math.log2(math.e)
REL = (0, 3, 1, 2)
F32, BF16 = jnp.float32, jnp.bfloat16


def ring(n, by):
    return [(i, (i + by) % n) for i in range(n)]


def head_step(a, by):
    return lax.ppermute(a, "head", ring(4, by))


def set_rows(meta_ref):
    y, c = meta_ref[2], meta_ref[3]
    blocks = []
    for swapped in (False, True):
        for k in range(4):
            blocks.append(lax.rem(y + REL[k], 4) * 2 + (1 - c if swapped else c))
    return blocks


def attend_kernel(section, *refs):
    meta_ref, xparts = refs[0], refs[1:9]
    masks, refs = (refs[9:10], refs[10:]) if section == 0 else (refs[9:11], refs[11:])
    gain_ref, other_gain_ref, wown, wparts, outs, refs = refs[0], refs[1], refs[2], refs[3:11], refs[11:15], refs[15:]
    if section == 0:
        v_ref, xs, q_s, k_s, u_s, w_s, s_s, a_s, sem = refs
    else:
        xs, q_s, k_s, u_s, w_s, s_s, a_s, sem = refs
    use_own = meta_ref[0] == section
    me = meta_ref[1]

    def own_copies():
        return [pltpu.make_async_copy(wown.at[j], w_s.at[:, pl.ds(j * FQ, FQ)], sem.at[j]) for j in range(3)]

    @pl.when(use_own)
    def _():
        for copy in own_copies():
            copy.start()

    @pl.when(jnp.logical_not(use_own))
    def _():
        for block, ref in zip(set_rows(meta_ref), wparts):
            for j in range(3):
                w_s[pl.ds(pl.multiple_of(block * 192, 192), 192), FQ * j : FQ * (j + 1)] = ref[j]

    if section == 0:
        for r in range(4):
            lanes = pl.ds(pl.multiple_of(lax.rem(me + REL[r], 4) * FQ, FQ), FQ)
            xs[0 : NT // 2, lanes] = xparts[2 * r][...]
            xs[NT // 2 : NT, lanes] = xparts[2 * r + 1][...]
        v_ref[...] = xs[pl.ds(pl.multiple_of(me * TS, TS), TS), :]
    gain = jnp.where(use_own, gain_ref[...], other_gain_ref[...])
    if section == 1:
        for i in range(8):
            xs[i * HALF : (i + 1) * HALF, :] = xparts[i][...]
    for h in range(HL):
        u_s[h, :, HD:] = jnp.ones((NT, HD), BF16)

    @pl.when(use_own)
    def _():
        for copy in own_copies():
            copy.wait()

    def make_qkv(i, carry):
        rows = pl.ds(pl.multiple_of(i * QROWS, QROWS), QROWS)
        x = xs[rows, :].astype(F32)
        ms = jnp.mean(x * x, axis=-1, keepdims=True)
        normed = (x * lax.rsqrt(ms + 1e-05) * gain).astype(BF16)
        acc = jnp.dot(normed, w_s[...], preferred_element_type=F32)
        for h in range(HL):
            q_s[h, rows, :] = (acc[:, HD * h : HD * (h + 1)] * QSCALE).astype(BF16)
            k_s[h, rows, :] = acc[:, FQ + HD * h : FQ + HD * (h + 1)].astype(BF16)
            u_s[h, rows, :HD] = acc[:, 2 * FQ + HD * h : 2 * FQ + HD * (h + 1)].astype(BF16)
        return carry

    lax.fori_loop(0, NT // QROWS, make_qkv, 0)

    def score(r, h):
        rows = pl.ds(pl.multiple_of(r * AROWS, AROWS), AROWS)
        s = lax.dot_general(q_s[h, rows, :], k_s[h], (((1,), (1,)), ((), ())), preferred_element_type=F32)
        if section == 0:
            return s + masks[0][...]
        return jnp.where(masks[1][rows, :] == masks[0][...], s, NEG)

    def weigh(r, h, s):
        rows = pl.ds(pl.multiple_of(r * AROWS, AROWS), AROWS)
        p = jnp.exp2(s - jnp.max(s, axis=-1, keepdims=True)).astype(BF16)
        o = jnp.dot(p, u_s[h], preferred_element_type=F32)
        a_s[rows, HD * h : HD * (h + 1)] = (o[:, :HD] / o[:, HD:]).astype(BF16)

    s_s[...] = score(0, 0)

    def attend_rows(r, carry):
        for h in range(HL):
            now = s_s[...]
            s_s[...] = score(r, h + 1) if h + 1 < HL else score(jnp.minimum(r + 1, NT // AROWS - 1), 0)
            weigh(r, h, now)
        return carry

    lax.fori_loop(0, NT // AROWS, attend_rows, 0)
    for r in range(4):
        if section == 0:
            outs[r][...] = a_s[pl.ds(pl.multiple_of(lax.rem(me + REL[r], 4) * TS, TS), TS), :]
        else:
            outs[r][...] = a_s[r * TS : (r + 1) * TS, :]


VM = pl.BlockSpec(memory_space=pltpu.VMEM)
SM = pl.BlockSpec(memory_space=pltpu.SMEM)


def attend(section, meta, pieces, masks, gains, wown, wparts):
    shard = jax.ShapeDtypeStruct((TS, FQ), BF16)
    out_shape = [shard] * 4 + ([jax.ShapeDtypeStruct((TS, D), BF16)] if section == 0 else [])
    scratch = [
        pltpu.VMEM((NT, D), BF16),
        pltpu.VMEM((HL, NT, HD), BF16),
        pltpu.VMEM((HL, NT, HD), BF16),
        pltpu.VMEM((HL, NT, 2 * HD), BF16),
        pltpu.VMEM((D, 3 * FQ), BF16),
        pltpu.VMEM((AROWS, NT), F32),
        pltpu.VMEM((NT, FQ), BF16),
        pltpu.SemaphoreType.DMA((3,)),
    ]
    return pl.pallas_call(
        functools.partial(attend_kernel, section),
        out_shape=out_shape,
        in_specs=[SM] + [VM] * (10 + len(masks)) + [pl.BlockSpec(memory_space=pltpu.HBM)] + [VM] * 8,
        out_specs=[VM] * len(out_shape),
        scratch_shapes=scratch,
        compiler_params=pltpu.CompilerParams(vmem_limit_bytes=30 << 20),
    )(meta, *pieces, *masks, *gains, pltpu.with_memory_space_constraint(wown, pltpu.HBM), *wparts)


def project_kernel(section, meta_ref, *refs):
    att, vparts, wparts = refs[:4], refs[4:6], refs[6:14]
    outs, (w_s, a_s, t_s) = refs[14:-3], refs[-3:]
    me = meta_ref[1]
    for block, ref in zip(set_rows(meta_ref), wparts):
        for r in range(4):
            w_s[pl.ds(pl.multiple_of(block * 48 + r * FQ, 16), 48), :] = ref[r]
    for r in range(4):
        a_s[:, r * FQ : (r + 1) * FQ] = att[r][...]
    acc = jnp.dot(a_s[...], w_s[...], preferred_element_type=F32)
    for i in range(2):
        rows = slice(i * HALF, (i + 1) * HALF)
        t_s[rows, :] = (acc[rows, :] + vparts[i][...].astype(F32)).astype(BF16)
        if section == 0:
            outs[i][...] = t_s[rows, :]
    for r in range(4):
        q = lax.rem(me + REL[r], 4)
        piece = t_s[:, pl.ds(pl.multiple_of(q * FQ, FQ), FQ)]
        outs[(2 if section == 0 else 0) + r][...] = piece


def project(section, meta, att, vparts, wparts):
    out_shape = [jax.ShapeDtypeStruct((TS, FQ), BF16)] * 4
    if section == 0:
        out_shape = [jax.ShapeDtypeStruct((HALF, D), BF16)] * 2 + out_shape
    return pl.pallas_call(
        functools.partial(project_kernel, section),
        out_shape=out_shape,
        in_specs=[SM] + [VM] * 14,
        out_specs=[VM] * len(out_shape),
        scratch_shapes=[pltpu.VMEM((D, D), BF16), pltpu.VMEM((TS, D), BF16), pltpu.VMEM((TS, D), BF16)],
        compiler_params=pltpu.CompilerParams(vmem_limit_bytes=20 << 20),
    )(meta, *att, *vparts, *wparts)


def gather_head(a, b):
    parts = {}
    for key, part, by in (("la", a, 1), ("lb", b, 1), ("ra", a, -1), ("rb", b, -1)):
        parts[key] = head_step(part, by)
    oa = head_step(parts["la"], 1)
    ob = head_step(parts["rb"], -1)
    return a, b, parts["la"], parts["lb"], parts["ra"], parts["rb"], oa, ob


def exchange_head(own, to_left, to_right, to_opp):
    from_left = head_step(to_right, 1)
    from_right = head_step(to_left, -1)
    from_opp = head_step(to_opp, 2)
    return own, from_left, from_right, from_opp


def pack_kernel(*refs):
    for i in range(4):
        refs[4][i] = refs[i][...]


def pack(parts):
    return pl.pallas_call(
        pack_kernel,
        out_shape=jax.ShapeDtypeStruct((4, *parts[0].shape), parts[0].dtype),
        in_specs=[VM] * 4,
        out_specs=VM,
        name="pack",
    )(*parts)


def win_step(a, by):
    return lax.ppermute(a, "win", ring(16, by))


def gather_win(own):
    mine = [own]
    for by in (4, -4, 8):
        mine.append(win_step(own, by))
    swapped = []
    for a in mine:
        swapped.append(lax.ppermute(a, "win", [(j, j ^ 1) for j in range(16)]))
    return mine + swapped


def slot_groups(a, fill):
    pad = [(0, 0), (0, 1)] + [(0, 0)] * (a.ndim - 2)
    return (
        a[:, 0:8],
        jnp.pad(a[:, 8:15], pad, constant_values=fill),
        a[:, 15:23],
        jnp.pad(a[:, 23:30], pad, constant_values=fill),
    )


FIRST, WIDTH = (0, 8, 15, 23), (8, 7, 8, 7)


def finish_kernel(meta_ref, *refs):
    near, distant, far, local, out, g_s = refs[0], refs[1], refs[2:6], refs[6:10], refs[10], refs[11]
    seg, me = meta_ref[0], meta_ref[1]

    @pl.when(seg == 0)
    def _():
        for r in range(4):
            g = lax.rem(me + REL[r], 4)
            g_s[0, g] = near[r]
            g_s[1, g] = distant[r]

    @pl.when(seg == 1)
    def _():
        for r in range(4):
            g = lax.rem(me + REL[r] + 2, 4)
            g_s[0, g] = far[r][...]
            g_s[1, g] = local[r][...]

    for m in range(2):
        for g in range(4):
            cells = g_s[m, g].reshape(30, 8, FQ)
            out[m, :, FIRST[g] : FIRST[g] + WIDTH[g], :] = cells[:, : WIDTH[g], :]


def finish(meta, near, distant, far, local):
    return pl.pallas_call(
        finish_kernel,
        out_shape=jax.ShapeDtypeStruct((2, 30, 30, FQ), BF16),
        in_specs=[SM] + [VM] * 10,
        out_specs=VM,
        scratch_shapes=[pltpu.VMEM((2, 4, TS, FQ), BF16)],
        name="finish",
    )(meta, near, distant, *far, *local)


def pair_perm(source, target, by):
    return [(source * 4 + i, target * 4 + (i + by) % 4) for i in range(4)]


def across(a, source, target, by):
    return lax.ppermute(a, ("segment", "head"), pair_perm(source, target, by))


def deliver(pieces, source, target):
    own, to_left, to_right, to_opp = pieces
    if source != target:
        own = across(own, source, target, 0)
    from_left = across(to_right, source, target, 1)
    from_right = across(to_left, source, target, -1)
    from_opp = across(to_opp, source, target, 2)
    return own, from_left, from_right, from_opp


def program(inputs, gains, qkv_weight, out_weight, labels):
    seg = lax.axis_index("segment")
    win = lax.axis_index("win")
    me = lax.axis_index("head")
    meta = jnp.stack([seg, me, win // 4, win % 2]).astype(jnp.int32)
    block = (win // 4) * 2 + win % 2

    wown = qkv_weight[0].transpose(1, 0, 2)
    wpart = lax.dynamic_slice_in_dim(wown, block * 192, 192, 1)
    wother = lax.ppermute(wpart, "segment", ring(2, 1))
    wparts = gather_win(wother)
    gains = (gains, lax.ppermute(gains, "segment", ring(2, 1)))
    opart = lax.dynamic_slice_in_dim(out_weight[0], block * 48, 48, 0)
    oown = jnp.stack(exchange_head(opart, opart, opart, opart))
    oother = lax.ppermute(oown, "segment", ring(2, 1))
    out0 = gather_win(jnp.where(seg == 0, oown, oother))
    out1 = gather_win(jnp.where(seg == 0, oother, oown))

    x = slot_groups(lax.dynamic_index_in_dim(inputs, seg, 0, keepdims=False), 0)
    xa, xb = jnp.concatenate(x[:2]).reshape(NT // 2, FQ), jnp.concatenate(x[2:]).reshape(NT // 2, FQ)
    slot = lax.broadcasted_iota(jnp.int32, (1, NT), 1)
    real = (slot % 8 != 7) | ((slot // TS) % 2 == 0)
    padr = jnp.where(real, 0.0, NEG).astype(F32)
    *att, v = attend(0, meta, gather_head(xa, xb), (padr,), gains, wown, wparts)
    att = exchange_head(*att)
    ta, tb, *fp = project(0, meta, att, (v[:HALF], v[HALF:]), out0)

    perm = [(((w + 1) % 16) * 4 + i, w * 4 + i) for w in range(16) for i in (0, 1)]
    ta = jnp.where(me < 2, lax.ppermute(ta, ("win", "head"), perm), ta)
    tb = jnp.where(me < 2, lax.ppermute(tb, ("win", "head"), perm), tb)
    lab = jnp.stack(slot_groups(labels.astype(F32), -1.0)).reshape(4, TS)
    lab = lax.dynamic_slice_in_dim(jnp.concatenate([lab] * 3), lax.rem(me + 2, 4), 4, 0)
    lab = jnp.stack([lab[0], lab[3], lab[1], lab[2]]).reshape(NT)
    att1 = attend(1, meta, gather_head(ta, tb), (lab[None, :], lab[:, None]), gains, wown, wparts)
    att1 = exchange_head(*att1)
    sp = project(1, meta, att1, (ta, tb), out1)

    near = pack(exchange_head(*fp))
    distant = across(near, 1, 0, 0)
    s_far = deliver(sp, 0, 1)
    s_local = deliver(sp, 1, 1)
    return finish(meta, near, distant, s_far, s_local)[None]


def solution(mesh):
    in_specs = (
        P(None, None, "win", "head"),
        P("segment", None),
        P("segment", None, None, "head"),
        P("segment", "head", None),
        P(None, "win"),
    )
    out_specs = P("segment", None, None, "win", "head")
    return jax.shard_map(program, mesh=mesh, in_specs=in_specs, out_specs=out_specs, check_vma=False)
```

```python
import functools
import math

import jax
import jax.numpy as jnp
from jax import lax
from jax.experimental import pallas as pl
from jax.experimental.pallas import tpu as pltpu
from jax.sharding import PartitionSpec as P


D = 1536
HD = 128
HL = 3
FQ = 384
TS = 240
NT = 4 * TS
HALF = TS // 2
QROWS = 480
AROWS = 480
NEG = -1e30
QSCALE = HD**-0.5 * math.log2(math.e)
REL = (0, 3, 1, 2)
F32, BF16 = jnp.float32, jnp.bfloat16


def ring(n, by):
    return [(i, (i + by) % n) for i in range(n)]


def head_step(a, by):
    return lax.ppermute(a, "head", ring(4, by))


def set_rows(meta_ref):
    y, c = meta_ref[2], meta_ref[3]
    blocks = []
    for swapped in (False, True):
        for k in range(4):
            blocks.append(lax.rem(y + REL[k], 4) * 2 + (1 - c if swapped else c))
    return blocks


def attend_kernel(section, *refs):
    meta_ref, xparts = refs[0], refs[1:9]
    masks, refs = (refs[9:10], refs[10:]) if section == 0 else (refs[9:13], refs[13:])
    gain_ref, other_gain_ref, wown, wparts, outs, refs = refs[0], refs[1], refs[2], refs[3:11], refs[11:15], refs[15:]
    if section == 0:
        v_ref, xs, q_s, k_s, u_s, w_s, s_s, a_s, sem = refs
    else:
        keep_ref, give_ref, xs, q_s, k_s, u_s, w_s, s_s, a_s, sem, g_s = refs
    use_own = meta_ref[0] == section
    me = meta_ref[1]

    def own_copies():
        return [pltpu.make_async_copy(wown.at[j], w_s.at[:, pl.ds(j * FQ, FQ)], sem.at[j]) for j in range(3)]

    @pl.when(use_own)
    def _():
        for copy in own_copies():
            copy.start()

    @pl.when(jnp.logical_not(use_own))
    def _():
        for block, ref in zip(set_rows(meta_ref), wparts):
            for j in range(3):
                w_s[pl.ds(pl.multiple_of(block * 192, 192), 192), FQ * j : FQ * (j + 1)] = ref[j]

    if section == 0:
        for r in range(4):
            lanes = pl.ds(pl.multiple_of(lax.rem(me + REL[r], 4) * FQ, FQ), FQ)
            xs[0 : NT // 2, lanes] = xparts[2 * r][...]
            xs[NT // 2 : NT, lanes] = xparts[2 * r + 1][...]
        v_ref[...] = xs[pl.ds(pl.multiple_of(me * TS, TS), TS), :]
    gain = jnp.where(use_own, gain_ref[...], other_gain_ref[...])
    if section == 1:
        for i in range(8):
            xs[i * HALF : (i + 1) * HALF, :] = xparts[i][...]

        @pl.when(me < 2)
        def _():
            for i in range(2):
                xs[i * HALF : (i + 1) * HALF, :] = masks[2 + i][...]

        lanes = pl.ds(pl.multiple_of(me * FQ, FQ), FQ)
        for r in range(4):
            g_s[lax.rem(me + REL[r], 4)] = xs[r * TS : (r + 1) * TS, lanes]
        give_ref[...] = g_s[:2]
        keep_ref[...] = g_s[2:]
    for h in range(HL):
        u_s[h, :, HD:] = jnp.ones((NT, HD), BF16)

    @pl.when(use_own)
    def _():
        for copy in own_copies():
            copy.wait()

    def make_qkv(i, carry):
        rows = pl.ds(pl.multiple_of(i * QROWS, QROWS), QROWS)
        x = xs[rows, :].astype(F32)
        ms = jnp.mean(x * x, axis=-1, keepdims=True)
        normed = (x * lax.rsqrt(ms + 1e-05) * gain).astype(BF16)
        acc = jnp.dot(normed, w_s[...], preferred_element_type=F32)
        for h in range(HL):
            q_s[h, rows, :] = (acc[:, HD * h : HD * (h + 1)] * QSCALE).astype(BF16)
            k_s[h, rows, :] = acc[:, FQ + HD * h : FQ + HD * (h + 1)].astype(BF16)
            u_s[h, rows, :HD] = acc[:, 2 * FQ + HD * h : 2 * FQ + HD * (h + 1)].astype(BF16)
        return carry

    lax.fori_loop(0, NT // QROWS, make_qkv, 0)

    def score(r, h):
        rows = pl.ds(pl.multiple_of(r * AROWS, AROWS), AROWS)
        s = lax.dot_general(q_s[h, rows, :], k_s[h], (((1,), (1,)), ((), ())), preferred_element_type=F32)
        if section == 0:
            return s + masks[0][...]
        return jnp.where(masks[1][rows, :] == masks[0][...], s, NEG)

    def weigh(r, h, s):
        rows = pl.ds(pl.multiple_of(r * AROWS, AROWS), AROWS)
        p = jnp.exp2(s - jnp.max(s, axis=-1, keepdims=True)).astype(BF16)
        o = jnp.dot(p, u_s[h], preferred_element_type=F32)
        a_s[rows, HD * h : HD * (h + 1)] = (o[:, :HD] / o[:, HD:]).astype(BF16)

    s_s[...] = score(0, 0)

    def attend_rows(r, carry):
        for h in range(HL):
            now = s_s[...]
            s_s[...] = score(r, h + 1) if h + 1 < HL else score(jnp.minimum(r + 1, NT // AROWS - 1), 0)
            weigh(r, h, now)
        return carry

    lax.fori_loop(0, NT // AROWS, attend_rows, 0)
    for r in range(4):
        if section == 0:
            outs[r][...] = a_s[pl.ds(pl.multiple_of(lax.rem(me + REL[r], 4) * TS, TS), TS), :]
        else:
            outs[r][...] = a_s[r * TS : (r + 1) * TS, :]


VM = pl.BlockSpec(memory_space=pltpu.VMEM)
SM = pl.BlockSpec(memory_space=pltpu.SMEM)


def attend(section, meta, pieces, masks, gains, wown, wparts):
    shard = jax.ShapeDtypeStruct((TS, FQ), BF16)
    if section == 0:
        out_shape = [shard] * 4 + [jax.ShapeDtypeStruct((TS, D), BF16)]
    else:
        out_shape = [shard] * 4 + [jax.ShapeDtypeStruct((2, TS, FQ), BF16)] * 2
    scratch = [
        pltpu.VMEM((NT, D), BF16),
        pltpu.VMEM((HL, NT, HD), BF16),
        pltpu.VMEM((HL, NT, HD), BF16),
        pltpu.VMEM((HL, NT, 2 * HD), BF16),
        pltpu.VMEM((D, 3 * FQ), BF16),
        pltpu.VMEM((AROWS, NT), F32),
        pltpu.VMEM((NT, FQ), BF16),
        pltpu.SemaphoreType.DMA((3,)),
    ]
    if section == 1:
        scratch += [pltpu.VMEM((4, TS, FQ), BF16)]
    return pl.pallas_call(
        functools.partial(attend_kernel, section),
        out_shape=out_shape,
        in_specs=[SM] + [VM] * (10 + len(masks)) + [pl.BlockSpec(memory_space=pltpu.HBM)] + [VM] * 8,
        out_specs=[VM] * len(out_shape),
        scratch_shapes=scratch,
        compiler_params=pltpu.CompilerParams(vmem_limit_bytes=30 << 20),
    )(meta, *pieces, *masks, *gains, pltpu.with_memory_space_constraint(wown, pltpu.HBM), *wparts)


def project_kernel(section, meta_ref, *refs):
    n = 6 if section == 0 else 8
    att, vparts, wparts = refs[:4], refs[4:n], refs[n : n + 8]
    outs, (w_s, a_s, t_s) = refs[n + 8 : -3], refs[-3:]
    me = meta_ref[1]
    for block, ref in zip(set_rows(meta_ref), wparts):
        for r in range(4):
            w_s[pl.ds(pl.multiple_of(block * 48 + r * FQ, 16), 48), :] = ref[r]
    for r in range(4):
        a_s[:, r * FQ : (r + 1) * FQ] = att[r][...]
    acc = jnp.dot(a_s[...], w_s[...], preferred_element_type=F32)
    for i in range(2):
        rows = slice(i * HALF, (i + 1) * HALF)
        v = vparts[i][...].astype(F32)
        if section == 1:
            v = jnp.where(me < 2, vparts[2 + i][...].astype(F32), v)
        t_s[rows, :] = (acc[rows, :] + v).astype(BF16)
        if section == 0:
            outs[i][...] = t_s[rows, :]
    if section == 1:
        for r in range(4):
            q = lax.rem(me + REL[r], 4)
            outs[r][...] = t_s[:, pl.ds(pl.multiple_of(q * FQ, FQ), FQ)]


def project(section, meta, att, vparts, wparts):
    if section == 0:
        out_shape = [jax.ShapeDtypeStruct((HALF, D), BF16)] * 2
    else:
        out_shape = [jax.ShapeDtypeStruct((TS, FQ), BF16)] * 4
    return pl.pallas_call(
        functools.partial(project_kernel, section),
        out_shape=out_shape,
        in_specs=[SM] + [VM] * (12 + len(vparts)),
        out_specs=[VM] * len(out_shape),
        scratch_shapes=[pltpu.VMEM((D, D), BF16), pltpu.VMEM((TS, D), BF16), pltpu.VMEM((TS, D), BF16)],
        compiler_params=pltpu.CompilerParams(vmem_limit_bytes=20 << 20),
    )(meta, *att, *vparts, *wparts)


def gather_head(a, b, step):
    parts = {}
    for key, part, by in (("la", a, 1), ("lb", b, 1), ("ra", a, -1), ("rb", b, -1)):
        parts[key] = step(part, by)
    oa = head_step(parts["la"], 1)
    ob = head_step(parts["rb"], -1)
    return parts["la"], parts["lb"], parts["ra"], parts["rb"], oa, ob


def exchange_head(own, to_left, to_right, to_opp):
    from_left = head_step(to_right, 1)
    from_right = head_step(to_left, -1)
    from_opp = head_step(to_opp, 2)
    return own, from_left, from_right, from_opp


def win_step(a, by):
    return lax.ppermute(a, "win", ring(16, by))


def gather_win(own):
    mine = [own]
    for by in (4, -4, 8):
        mine.append(win_step(own, by))
    swapped = []
    for a in mine:
        swapped.append(lax.ppermute(a, "win", [(j, j ^ 1) for j in range(16)]))
    return mine + swapped


def slot_groups(a, fill):
    pad = [(0, 0), (0, 1)] + [(0, 0)] * (a.ndim - 2)
    return (
        a[:, 0:8],
        jnp.pad(a[:, 8:15], pad, constant_values=fill),
        a[:, 15:23],
        jnp.pad(a[:, 23:30], pad, constant_values=fill),
    )


FIRST, WIDTH = (0, 8, 15, 23), (8, 7, 8, 7)


def finish_kernel(meta_ref, *refs):
    near, distant, far, local, out, g_s = refs[:2], refs[2:4], refs[4:8], refs[8:12], refs[12], refs[13]
    seg, me = meta_ref[0], meta_ref[1]

    @pl.when(seg == 0)
    def _():
        for i in range(2):
            g_s[0, 2 * i : 2 * i + 2] = near[i][...]
            g_s[1, 2 * i : 2 * i + 2] = distant[i][...]

    @pl.when(seg == 1)
    def _():
        for r in range(4):
            g = lax.rem(me + REL[r] + 2, 4)
            g_s[0, g] = far[r][...]
            g_s[1, g] = local[r][...]

    for m in range(2):
        for g in range(4):
            cells = g_s[m, g].reshape(30, 8, FQ)
            out[m, :, FIRST[g] : FIRST[g] + WIDTH[g], :] = cells[:, : WIDTH[g], :]


def finish(meta, near, distant, far, local):
    return pl.pallas_call(
        finish_kernel,
        out_shape=jax.ShapeDtypeStruct((2, 30, 30, FQ), BF16),
        in_specs=[SM] + [VM] * 12,
        out_specs=VM,
        scratch_shapes=[pltpu.VMEM((2, 4, TS, FQ), BF16)],
        name="finish",
    )(meta, *near, *distant, *far, *local)


def pair_perm(source, target, by):
    return [(source * 4 + i, target * 4 + (i + by) % 4) for i in range(4)]


def across(a, source, target, by):
    return lax.ppermute(a, ("segment", "head"), pair_perm(source, target, by))


def deliver(pieces, source, target):
    own, to_left, to_right, to_opp = pieces
    if source != target:
        own = across(own, source, target, 0)
    from_left = across(to_right, source, target, 1)
    from_right = across(to_left, source, target, -1)
    from_opp = across(to_opp, source, target, 2)
    return own, from_left, from_right, from_opp


def program(inputs, gains, qkv_weight, out_weight, labels):
    seg = lax.axis_index("segment")
    win = lax.axis_index("win")
    me = lax.axis_index("head")
    meta = jnp.stack([seg, me, win // 4, win % 2]).astype(jnp.int32)
    block = (win // 4) * 2 + win % 2

    wown = qkv_weight[0].transpose(1, 0, 2)
    wpart = lax.dynamic_slice_in_dim(wown, block * 192, 192, 1)
    wother = lax.ppermute(wpart, "segment", ring(2, 1))
    wparts = gather_win(wother)
    gains = (gains, lax.ppermute(gains, "segment", ring(2, 1)))
    opart = lax.dynamic_slice_in_dim(out_weight[0], block * 48, 48, 0)
    oown = jnp.stack(exchange_head(opart, opart, opart, opart))
    oother = lax.ppermute(oown, "segment", ring(2, 1))
    out0 = gather_win(jnp.where(seg == 0, oown, oother))
    out1 = gather_win(jnp.where(seg == 0, oother, oown))

    x = slot_groups(lax.dynamic_index_in_dim(inputs, seg, 0, keepdims=False), 0)
    xa, xb = jnp.concatenate(x[:2]).reshape(NT // 2, FQ), jnp.concatenate(x[2:]).reshape(NT // 2, FQ)
    slot = lax.broadcasted_iota(jnp.int32, (1, NT), 1)
    real = (slot % 8 != 7) | ((slot // TS) % 2 == 0)
    padr = jnp.where(real, 0.0, NEG).astype(F32)
    *att, v = attend(0, meta, (xa, xb, *gather_head(xa, xb, head_step)), (padr,), gains, wown, wparts)
    att = exchange_head(*att)
    ta, tb = project(0, meta, att, (v[:HALF], v[HALF:]), out0)

    def source(w, i):
        return ((w + 1) % 16 if i < 2 else w) * 4 + i

    def shifted_step(part, by):
        perm = [(source(w, i), w * 4 + (i + by) % 4) for w in range(16) for i in range(4)]
        return lax.ppermute(part, ("win", "head"), perm)

    others = gather_head(ta, tb, shifted_step)
    perm = [(source(w, i), w * 4 + i) for w in range(16) for i in (0, 1)]
    sa = lax.ppermute(ta, ("win", "head"), perm)
    sb = lax.ppermute(tb, ("win", "head"), perm)
    lab = jnp.stack(slot_groups(labels.astype(F32), -1.0)).reshape(4, TS)
    lab = lax.dynamic_slice_in_dim(jnp.concatenate([lab] * 3), lax.rem(me + 2, 4), 4, 0)
    lab = jnp.stack([lab[0], lab[3], lab[1], lab[2]]).reshape(NT)
    *att1, keep, give = attend(1, meta, (ta, tb, *others), (lab[None, :], lab[:, None], sa, sb), gains, wown, wparts)
    att1 = exchange_head(*att1)
    sp = project(1, meta, att1, (ta, tb, sa, sb), out1)

    onward = [(w, (w + 1) % 16) for w in range(16)]
    near = lax.ppermute(give, ("segment", "win"), onward)
    far_keep = lax.ppermute(keep, "segment", [(1, 0)])
    far_give = lax.ppermute(give, ("segment", "win"), [(16 + w, v) for w, v in onward])
    s_far = deliver(sp, 0, 1)
    s_local = deliver(sp, 1, 1)
    return finish(meta, (near, keep), (far_give, far_keep), s_far, s_local)[None]


def solution(mesh):
    in_specs = (
        P(None, None, "win", "head"),
        P("segment", None),
        P("segment", None, None, "head"),
        P("segment", "head", None),
        P(None, "win"),
    )
    out_specs = P("segment", None, None, "win", "head")
    return jax.shard_map(program, mesh=mesh, in_specs=in_specs, out_specs=out_specs, check_vma=False)
```

```python
import functools
import math

import jax
import jax.numpy as jnp
from jax import lax
from jax.experimental import pallas as pl
from jax.experimental.pallas import tpu as pltpu
from jax.sharding import PartitionSpec as P


D = 1536
HD = 128
HL = 3
FQ = 384
TS = 240
NT = 4 * TS
HALF = TS // 2
QROWS = 480
AROWS = 480
NEG = -1e30
QSCALE = HD**-0.5 * math.log2(math.e)
REL = (0, 3, 1, 2)
F32, BF16 = jnp.float32, jnp.bfloat16


def ring(n, by):
    return [(i, (i + by) % n) for i in range(n)]


def head_step(a, by):
    return lax.ppermute(a, "head", ring(4, by))


def set_rows(meta_ref):
    y, c = meta_ref[2], meta_ref[3]
    blocks = []
    for swapped in (False, True):
        for k in range(4):
            blocks.append(lax.rem(y + REL[k], 4) * 2 + (1 - c if swapped else c))
    return blocks


def attend_kernel(section, *refs):
    meta_ref, xparts = refs[0], refs[1:9]
    masks, refs = (refs[9:10], refs[10:]) if section == 0 else (refs[9:11], refs[11:])
    gain_ref, other_gain_ref, wown, wparts, outs, refs = refs[0], refs[1], refs[2], refs[3:11], refs[11:15], refs[15:]
    if section == 0:
        v_ref, xs, q_s, k_s, u_s, w_s, s_s, a_s, sem = refs
    else:
        keep_ref, give_ref, xs, q_s, k_s, u_s, w_s, s_s, a_s, sem, g_s = refs
    use_own = meta_ref[0] == section
    me = meta_ref[1]

    def own_copies():
        return [pltpu.make_async_copy(wown.at[j], w_s.at[:, pl.ds(j * FQ, FQ)], sem.at[j]) for j in range(3)]

    @pl.when(use_own)
    def _():
        for copy in own_copies():
            copy.start()

    @pl.when(jnp.logical_not(use_own))
    def _():
        for block, ref in zip(set_rows(meta_ref), wparts):
            for j in range(3):
                w_s[pl.ds(pl.multiple_of(block * 192, 192), 192), FQ * j : FQ * (j + 1)] = ref[j]

    if section == 0:
        for r in range(4):
            lanes = pl.ds(pl.multiple_of(lax.rem(me + REL[r], 4) * FQ, FQ), FQ)
            xs[0 : NT // 2, lanes] = xparts[2 * r][...]
            xs[NT // 2 : NT, lanes] = xparts[2 * r + 1][...]
        v_ref[...] = xs[pl.ds(pl.multiple_of(me * TS, TS), TS), :]
    gain = jnp.where(use_own, gain_ref[...], other_gain_ref[...])
    if section == 1:
        for i in range(8):
            xs[i * HALF : (i + 1) * HALF, :] = xparts[i][...]
        lanes = pl.ds(pl.multiple_of(me * FQ, FQ), FQ)
        for r in range(4):
            g_s[lax.rem(me + REL[r], 4)] = xs[r * TS : (r + 1) * TS, lanes]
        give_ref[...] = g_s[:2]
        keep_ref[...] = g_s[2:]
    for h in range(HL):
        u_s[h, :, HD:] = jnp.ones((NT, HD), BF16)

    @pl.when(use_own)
    def _():
        for copy in own_copies():
            copy.wait()

    def make_qkv(i, carry):
        rows = pl.ds(pl.multiple_of(i * QROWS, QROWS), QROWS)
        x = xs[rows, :].astype(F32)
        ms = jnp.mean(x * x, axis=-1, keepdims=True)
        normed = (x * lax.rsqrt(ms + 1e-05) * gain).astype(BF16)
        acc = jnp.dot(normed, w_s[...], preferred_element_type=F32)
        for h in range(HL):
            q_s[h, rows, :] = (acc[:, HD * h : HD * (h + 1)] * QSCALE).astype(BF16)
            k_s[h, rows, :] = acc[:, FQ + HD * h : FQ + HD * (h + 1)].astype(BF16)
            u_s[h, rows, :HD] = acc[:, 2 * FQ + HD * h : 2 * FQ + HD * (h + 1)].astype(BF16)
        return carry

    lax.fori_loop(0, NT // QROWS, make_qkv, 0)

    def score(r, h):
        rows = pl.ds(pl.multiple_of(r * AROWS, AROWS), AROWS)
        s = lax.dot_general(q_s[h, rows, :], k_s[h], (((1,), (1,)), ((), ())), preferred_element_type=F32)
        if section == 0:
            return s + masks[0][...]
        return jnp.where(masks[1][rows, :] == masks[0][...], s, NEG)

    def weigh(r, h, s):
        rows = pl.ds(pl.multiple_of(r * AROWS, AROWS), AROWS)
        p = jnp.exp2(s - jnp.max(s, axis=-1, keepdims=True)).astype(BF16)
        o = jnp.dot(p, u_s[h], preferred_element_type=F32)
        a_s[rows, HD * h : HD * (h + 1)] = (o[:, :HD] / o[:, HD:]).astype(BF16)

    s_s[...] = score(0, 0)

    def attend_rows(r, carry):
        for h in range(HL):
            now = s_s[...]
            s_s[...] = score(r, h + 1) if h + 1 < HL else score(jnp.minimum(r + 1, NT // AROWS - 1), 0)
            weigh(r, h, now)
        return carry

    lax.fori_loop(0, NT // AROWS, attend_rows, 0)
    for r in range(4):
        if section == 0:
            outs[r][...] = a_s[pl.ds(pl.multiple_of(lax.rem(me + REL[r], 4) * TS, TS), TS), :]
        else:
            outs[r][...] = a_s[r * TS : (r + 1) * TS, :]


VM = pl.BlockSpec(memory_space=pltpu.VMEM)
SM = pl.BlockSpec(memory_space=pltpu.SMEM)


def attend(section, meta, pieces, masks, gains, wown, wparts):
    shard = jax.ShapeDtypeStruct((TS, FQ), BF16)
    if section == 0:
        out_shape = [shard] * 4 + [jax.ShapeDtypeStruct((TS, D), BF16)]
    else:
        out_shape = [shard] * 4 + [jax.ShapeDtypeStruct((2, TS, FQ), BF16)] * 2
    scratch = [
        pltpu.VMEM((NT, D), BF16),
        pltpu.VMEM((HL, NT, HD), BF16),
        pltpu.VMEM((HL, NT, HD), BF16),
        pltpu.VMEM((HL, NT, 2 * HD), BF16),
        pltpu.VMEM((D, 3 * FQ), BF16),
        pltpu.VMEM((AROWS, NT), F32),
        pltpu.VMEM((NT, FQ), BF16),
        pltpu.SemaphoreType.DMA((3,)),
    ]
    if section == 1:
        scratch += [pltpu.VMEM((4, TS, FQ), BF16)]
    return pl.pallas_call(
        functools.partial(attend_kernel, section),
        out_shape=out_shape,
        in_specs=[SM] + [VM] * (10 + len(masks)) + [pl.BlockSpec(memory_space=pltpu.HBM)] + [VM] * 8,
        out_specs=[VM] * len(out_shape),
        scratch_shapes=scratch,
        compiler_params=pltpu.CompilerParams(vmem_limit_bytes=30 << 20),
    )(meta, *pieces, *masks, *gains, pltpu.with_memory_space_constraint(wown, pltpu.HBM), *wparts)


def project_kernel(section, meta_ref, *refs):
    att, vparts, wparts = refs[:4], refs[4:6], refs[6:14]
    outs, (w_s, a_s, t_s) = refs[14:-3], refs[-3:]
    me = meta_ref[1]
    for block, ref in zip(set_rows(meta_ref), wparts):
        for r in range(4):
            w_s[pl.ds(pl.multiple_of(block * 48 + r * FQ, 16), 48), :] = ref[r]
    for r in range(4):
        a_s[:, r * FQ : (r + 1) * FQ] = att[r][...]
    acc = jnp.dot(a_s[...], w_s[...], preferred_element_type=F32)
    for i in range(2):
        rows = slice(i * HALF, (i + 1) * HALF)
        t_s[rows, :] = (acc[rows, :] + vparts[i][...].astype(F32)).astype(BF16)
        if section == 0:
            outs[i][...] = t_s[rows, :]
    if section == 1:
        for r in range(4):
            q = lax.rem(me + REL[r], 4)
            outs[r][...] = t_s[:, pl.ds(pl.multiple_of(q * FQ, FQ), FQ)]


def project(section, meta, att, vparts, wparts):
    if section == 0:
        out_shape = [jax.ShapeDtypeStruct((HALF, D), BF16)] * 2
    else:
        out_shape = [jax.ShapeDtypeStruct((TS, FQ), BF16)] * 4
    return pl.pallas_call(
        functools.partial(project_kernel, section),
        out_shape=out_shape,
        in_specs=[SM] + [VM] * 14,
        out_specs=[VM] * len(out_shape),
        scratch_shapes=[pltpu.VMEM((D, D), BF16), pltpu.VMEM((TS, D), BF16), pltpu.VMEM((TS, D), BF16)],
        compiler_params=pltpu.CompilerParams(vmem_limit_bytes=20 << 20),
    )(meta, *att, *vparts, *wparts)


def gather_head(a, b, step):
    parts = {}
    for key, part, by in (("la", a, 1), ("lb", b, 1), ("ra", a, -1), ("rb", b, -1)):
        parts[key] = step(part, by)
    oa = head_step(parts["la"], 1)
    ob = head_step(parts["rb"], -1)
    return parts["la"], parts["lb"], parts["ra"], parts["rb"], oa, ob


def exchange_head(own, to_left, to_right, to_opp):
    from_left = head_step(to_right, 1)
    from_right = head_step(to_left, -1)
    from_opp = head_step(to_opp, 2)
    return own, from_left, from_right, from_opp


def win_step(a, by):
    return lax.ppermute(a, "win", ring(16, by))


def gather_win(own):
    mine = [own]
    for by in (4, -4, 8):
        mine.append(win_step(own, by))
    swapped = []
    for a in mine:
        swapped.append(lax.ppermute(a, "win", [(j, j ^ 1) for j in range(16)]))
    return mine + swapped


def slot_groups(a, fill):
    pad = [(0, 0), (0, 1)] + [(0, 0)] * (a.ndim - 2)
    return (
        a[:, 0:8],
        jnp.pad(a[:, 8:15], pad, constant_values=fill),
        a[:, 15:23],
        jnp.pad(a[:, 23:30], pad, constant_values=fill),
    )


FIRST, WIDTH = (0, 8, 15, 23), (8, 7, 8, 7)


def finish_kernel(meta_ref, *refs):
    near, distant, far, local, out, g_s = refs[:2], refs[2:4], refs[4:8], refs[8:12], refs[12], refs[13]
    seg, me = meta_ref[0], meta_ref[1]

    @pl.when(seg == 0)
    def _():
        for i in range(2):
            g_s[0, 2 * i : 2 * i + 2] = near[i][...]
            g_s[1, 2 * i : 2 * i + 2] = distant[i][...]

    @pl.when(seg == 1)
    def _():
        for r in range(4):
            g = lax.rem(me + REL[r] + 2, 4)
            g_s[0, g] = far[r][...]
            g_s[1, g] = local[r][...]

    for m in range(2):
        for g in range(4):
            cells = g_s[m, g].reshape(30, 8, FQ)
            out[m, :, FIRST[g] : FIRST[g] + WIDTH[g], :] = cells[:, : WIDTH[g], :]


def finish(meta, near, distant, far, local):
    return pl.pallas_call(
        finish_kernel,
        out_shape=jax.ShapeDtypeStruct((2, 30, 30, FQ), BF16),
        in_specs=[SM] + [VM] * 12,
        out_specs=VM,
        scratch_shapes=[pltpu.VMEM((2, 4, TS, FQ), BF16)],
        name="finish",
    )(meta, *near, *distant, *far, *local)


def pair_perm(source, target, by):
    return [(source * 4 + i, target * 4 + (i + by) % 4) for i in range(4)]


def across(a, source, target, by):
    return lax.ppermute(a, ("segment", "head"), pair_perm(source, target, by))


def deliver(pieces, source, target):
    own, to_left, to_right, to_opp = pieces
    if source != target:
        own = across(own, source, target, 0)
    from_left = across(to_right, source, target, 1)
    from_right = across(to_left, source, target, -1)
    from_opp = across(to_opp, source, target, 2)
    return own, from_left, from_right, from_opp


def program(inputs, gains, qkv_weight, out_weight, labels):
    seg = lax.axis_index("segment")
    win = lax.axis_index("win")
    me = lax.axis_index("head")
    meta = jnp.stack([seg, me, win // 4, win % 2]).astype(jnp.int32)
    block = (win // 4) * 2 + win % 2

    wown = qkv_weight[0].transpose(1, 0, 2)
    wpart = lax.dynamic_slice_in_dim(wown, block * 192, 192, 1)
    wother = lax.ppermute(wpart, "segment", ring(2, 1))
    wparts = gather_win(wother)
    gains = (gains, lax.ppermute(gains, "segment", ring(2, 1)))
    opart = lax.dynamic_slice_in_dim(out_weight[0], block * 48, 48, 0)
    oown = jnp.stack(exchange_head(opart, opart, opart, opart))
    oother = lax.ppermute(oown, "segment", ring(2, 1))
    out0 = gather_win(jnp.where(seg == 0, oown, oother))
    out1 = gather_win(jnp.where(seg == 0, oother, oown))

    x = slot_groups(lax.dynamic_index_in_dim(inputs, seg, 0, keepdims=False), 0)
    xa, xb = jnp.concatenate(x[:2]).reshape(NT // 2, FQ), jnp.concatenate(x[2:]).reshape(NT // 2, FQ)
    slot = lax.broadcasted_iota(jnp.int32, (1, NT), 1)
    real = (slot % 8 != 7) | ((slot // TS) % 2 == 0)
    padr = jnp.where(real, 0.0, NEG).astype(F32)
    *att, v = attend(0, meta, (xa, xb, *gather_head(xa, xb, head_step)), (padr,), gains, wown, wparts)
    att = exchange_head(*att)
    ta, tb = project(0, meta, att, (v[:HALF], v[HALF:]), out0)

    def source(w, i):
        return ((w + 1) % 16 if i < 2 else w) * 4 + i

    def shifted_step(part, by):
        perm = [(source(w, i), w * 4 + (i + by) % 4) for w in range(16) for i in range(4)]
        return lax.ppermute(part, ("win", "head"), perm)

    others = gather_head(ta, tb, shifted_step)
    perm = [(source(w, i), w * 4 + i) for w in range(16) for i in (0, 1)]
    ta = jnp.where(me < 2, lax.ppermute(ta, ("win", "head"), perm), ta)
    tb = jnp.where(me < 2, lax.ppermute(tb, ("win", "head"), perm), tb)
    lab = jnp.stack(slot_groups(labels.astype(F32), -1.0)).reshape(4, TS)
    lab = lax.dynamic_slice_in_dim(jnp.concatenate([lab] * 3), lax.rem(me + 2, 4), 4, 0)
    lab = jnp.stack([lab[0], lab[3], lab[1], lab[2]]).reshape(NT)
    *att1, keep, give = attend(1, meta, (ta, tb, *others), (lab[None, :], lab[:, None]), gains, wown, wparts)
    att1 = exchange_head(*att1)
    sp = project(1, meta, att1, (ta, tb), out1)

    onward = [(w, (w + 1) % 16) for w in range(16)]
    near = lax.ppermute(give, ("segment", "win"), onward)
    far_keep = lax.ppermute(keep, "segment", [(1, 0)])
    far_give = lax.ppermute(give, ("segment", "win"), [(16 + w, v) for w, v in onward])
    s_far = deliver(sp, 0, 1)
    s_local = deliver(sp, 1, 1)
    return finish(meta, (near, keep), (far_give, far_keep), s_far, s_local)[None]


def solution(mesh):
    in_specs = (
        P(None, None, "win", "head"),
        P("segment", None),
        P("segment", None, None, "head"),
        P("segment", "head", None),
        P(None, "win"),
    )
    out_specs = P("segment", None, None, "win", "head")
    return jax.shard_map(program, mesh=mesh, in_specs=in_specs, out_specs=out_specs, check_vma=False)
```
